256 devices in a mesh: dp: 64 (over y, z_lo, x), ctx: 4 (over z_hi, core).
Axes of the slice: x: 4, y: 4, z: 8 (z_hi: 2, z_lo: 4; z = z_hi * 4 + z_lo), core: 2. Of those that a mesh axis runs over, the one named last changes fastest.
Arguments:
- hidden: bfloat16 [64, 512, 3584], P('dp', 'ctx'), may hold values from -6 to 6
- norm_gain: bfloat16 [3584], replicated, may hold values from 0.099609375 to 1.8984375
- w_query: bfloat16 [3584, 2048], P('dp'), may hold values from -0.09375 to 0.09375
- w_key: bfloat16 [3584, 512], P('dp'), may hold values from -0.09375 to 0.09375
- w_value: bfloat16 [3584, 512], P('dp'), may hold values from -0.09375 to 0.09375
- bias_query: bfloat16 [2048], replicated, may hold values from -4 to 4
- bias_key: bfloat16 [512], replicated, may hold values from -4 to 4
- bias_value: bfloat16 [512], replicated, may hold values from -4 to 4
- kv_blocks: int32 [16, 4, 4], P('ctx'), may hold values from 0 to 3, as said below
- block_counts: int32 [16, 4], P('ctx'), may hold values from 1 to 4, as said below
Outputs:
- attended: bfloat16 [64, 512, 2048], P('dp', 'ctx')
The draws below stay inside these ranges and needn't reach their ends.
Inputs may be any that keep to these rules, and one draw needn't show every extreme that they name: Entry 0 of kv_blocks[h, b] is b itself; entries 1 to block_counts[h, b] - 1 are distinct blocks below b; later entries are valid block numbers that are not used. block_counts[h, b] is at most b + 1, and the last query block of every head has 4.
All inputs are finite; a program needn't handle non-finite values.
Results may differ from the reference program's by a relative error of at most 0.0053.
Values may be sent and summed in bfloat16 or wider, within the bound.
No kernel may reach another device: no remote copies, remote signals or barrier semaphores. Data moves between devices by JAX's collectives and lax.ppermute only.
A program may use at most 64 MiB of HBM per device.

```python
import jax
import jax.numpy as jnp
from jax import lax

D = 3584
KVH = 4
HEAD = 128
QHEADS = 16
BLOCK = 128
MAXB = 4
SEQ = 512
QBLOCKS = 4
DOCS = 64


def mask_tables(key):
    level_key, slot_key, count_key = jax.random.split(jax.random.fold_in(key, 7), 3)
    levels = jax.random.randint(level_key, (QHEADS, 1), 0, MAXB)
    raw_counts = jax.random.randint(count_key, (QHEADS, QBLOCKS), 0, MAXB)
    rows_idx = jnp.arange(QBLOCKS)
    counts = jnp.minimum(1 + jnp.minimum(raw_counts, levels), rows_idx[None, :] + 1)
    counts = jnp.where(rows_idx[None, :] == QBLOCKS - 1, MAXB, counts)
    noise = jax.random.randint(slot_key, (QHEADS, QBLOCKS, QBLOCKS), 0, 1 << 20)
    cols_idx = jnp.arange(QBLOCKS)
    below = cols_idx[None, None, :] < rows_idx[None, :, None]
    scored = jnp.where(below, noise * QBLOCKS + cols_idx[None, None, :], (1 << 20) * QBLOCKS + cols_idx[None, None, :])
    order = jnp.argsort(scored, axis=-1, stable=True)[..., :MAXB - 1]
    usable = jnp.arange(MAXB - 1)[None, :] < rows_idx[:, None]
    others = jnp.where(usable[None, :, :], order, rows_idx[None, :, None])
    diagonal = jnp.broadcast_to(rows_idx[None, :, None], (QHEADS, QBLOCKS, 1))
    blocks = jnp.concatenate([diagonal, others], axis=-1)
    return (blocks.astype(jnp.int32), counts.astype(jnp.int32))


def draw_kv_blocks(key, part):
    return mask_tables(key)[0]


def draw_block_counts(key, part):
    return mask_tables(key)[1]


def level_of(own_key, dims, cuts, smallest, top_value):
    loudness = 1.0
    for dim, shards_of in cuts:
        steps = jax.random.uniform(jax.random.fold_in(jax.random.fold_in(own_key, 6), dim), (shards_of,), jnp.float32, smallest / len(cuts), top_value / len(cuts))
        loudness = loudness * jnp.repeat(jnp.exp(steps), dims[dim] // shards_of).reshape((-1,) + (1,) * (len(dims) - 1 - dim))
    return loudness


def bell_draw(stream_key, dims, deviation, reach, cuts=(), kind=jnp.bfloat16):
    gain = level_of(stream_key, dims, cuts, -0.22, 0.18) if cuts else 1.0
    result = jax.random.normal(stream_key, dims, jnp.float32) * deviation * gain
    return jnp.minimum(jnp.maximum(result, -reach), reach).astype(kind)


def setup_inputs(seed: int = 0) -> dict:
    key_of = jax.random.split(jax.random.key(seed), 11)
    hidden = bell_draw(key_of[0], (DOCS, SEQ, D), 1.0, 6.0, ((0, 64), (1, 4)))
    norm_gain = jnp.clip(1.0 + 0.18 * jax.random.normal(key_of[1], (D,), jnp.float32), 0.099609375, 1.8984375).astype(jnp.bfloat16)
    w_query = bell_draw(key_of[2], (D, QHEADS * HEAD), D ** -0.5, 0.09375, ((0, 64),))
    w_key = bell_draw(key_of[3], (D, KVH * HEAD), D ** -0.5, 0.09375, ((0, 64),))
    w_value = bell_draw(key_of[4], (D, KVH * HEAD), D ** -0.5, 0.09375, ((0, 64),))
    bias_query = bell_draw(key_of[5], (QHEADS * HEAD,), 1.0, 4.0)
    bias_key = bell_draw(key_of[6], (KVH * HEAD,), 1.0, 4.0)
    bias_value = bell_draw(key_of[7], (KVH * HEAD,), 1.0, 4.0)
    kv_blocks = draw_kv_blocks(jax.random.fold_in(key_of[10], 71), 0)
    block_counts = draw_block_counts(jax.random.fold_in(key_of[10], 71), 0)
    return {"hidden": hidden, "norm_gain": norm_gain, "w_query": w_query, "w_key": w_key, "w_value": w_value, "bias_query": bias_query, "bias_key": bias_key, "bias_value": bias_value, "kv_blocks": kv_blocks, "block_counts": block_counts}


EPSILON = 1e-06
THETA = 1000000.0

def rms_norm(tokens, norm_gain):
    floats = tokens.astype(jnp.float32)
    meansq = lax.optimization_barrier(jnp.mean(floats * floats, axis=-1, keepdims=True))
    return (floats * lax.rsqrt(meansq + EPSILON) * norm_gain.astype(jnp.float32)).astype(jnp.bfloat16)

def rotary(heads_in, position):
    half_size = heads_in.shape[-1] // 2
    exponent = jnp.arange(half_size, dtype=jnp.float32) * (2.0 / heads_in.shape[-1])
    inverse = jnp.power(jnp.float32(THETA), -exponent)
    angles = position[:, None] * inverse[None, :]
    cosine = jnp.cos(angles)[:, None, :]
    sine = jnp.sin(angles)[:, None, :]
    first = heads_in[..., :half_size]
    second = heads_in[..., half_size:]
    return jnp.concatenate([first * cosine - second * sine, second * cosine + first * sine], axis=-1)

def head_projection(normed, weight, bias, heads, position, rotate_it):
    summed = jnp.dot(normed, weight, preferred_element_type=jnp.float32) + bias.astype(jnp.float32)
    shaped = summed.reshape(summed.shape[0], heads, HEAD)
    if rotate_it:
        shaped = rotary(shaped, position)
    return shaped.astype(jnp.bfloat16)

def sparse_head(queries, key_rows, value_rows, blocks, counts):
    nblocks = queries.shape[0] // BLOCK
    query_tiles = queries.reshape(nblocks, BLOCK, HEAD)
    key_tiles = key_rows.reshape(nblocks, BLOCK, HEAD)[blocks].reshape(nblocks, MAXB * BLOCK, HEAD)
    value_tiles = value_rows.reshape(nblocks, BLOCK, HEAD)[blocks].reshape(nblocks, MAXB * BLOCK, HEAD)
    scores = jnp.einsum('qih,qjh->qij', query_tiles.astype(jnp.float32), key_tiles.astype(jnp.float32)) * HEAD ** (-0.5)
    column = jnp.arange(MAXB * BLOCK)
    slot_of = column // BLOCK
    inside = column % BLOCK
    row_pos = jnp.arange(BLOCK)
    allowed = (slot_of[None, None, :] < counts[:, None, None]) & ((slot_of[None, None, :] > 0) | (inside[None, None, :] <= row_pos[None, :, None]))
    expo = jnp.where(allowed, jnp.exp(scores), jnp.float32(0.0))
    totals = lax.optimization_barrier(jnp.sum(expo, axis=-1))
    probs = expo.astype(jnp.bfloat16)
    mixed = jnp.einsum('qij,qjh->qih', probs.astype(jnp.float32), value_tiles.astype(jnp.float32)) / totals[..., None]
    return mixed.astype(jnp.bfloat16).reshape(nblocks * BLOCK, HEAD)

def reference(hidden, norm_gain, w_query, w_key, w_value, bias_query, bias_key, bias_value, kv_blocks, block_counts):
    group = QHEADS // KVH
    position = jnp.arange(SEQ, dtype=jnp.float32)

    def one_head(packed):
        return sparse_head(packed[0], packed[1], packed[2], packed[3], packed[4])

    def one_document(tokens):
        normed = rms_norm(tokens, norm_gain)
        queries = head_projection(normed, w_query, bias_query, QHEADS, position, True)
        key_rows = jnp.repeat(head_projection(normed, w_key, bias_key, KVH, position, True), group, axis=1)
        value_rows = jnp.repeat(head_projection(normed, w_value, bias_value, KVH, position, False), group, axis=1)
        mixed = lax.map(one_head, (queries.transpose(1, 0, 2), key_rows.transpose(1, 0, 2), value_rows.transpose(1, 0, 2), kv_blocks, block_counts))
        return mixed.transpose(1, 0, 2).reshape(SEQ, QHEADS * HEAD)
    return lax.map(one_document, hidden)
```

```python
import functools

import jax
import jax.numpy as jnp
import numpy as np
from jax import lax
from jax.experimental import pallas as pl
from jax.experimental.pallas import tpu as pltpu
from jax.sharding import Mesh
from jax.sharding import PartitionSpec as P

KVH = 4
HEAD = 128
QHEADS = 16
BLOCK = 128
MAXB = 4
EPSILON = 1e-06
THETA = 1000000.0

AXES = ("y", "zl", "x", "zh", "core")
OFFSETS = (0, -1, 1, 2)
DOC = ("y", "zl", "x")
CTX = ("zh", "core")


def z_index(z):
    return (z % 4) * 2 + (z % 8) // 4


def plane_perm(first, shift):
    pairs = []
    for y in range(4):
        for x in range(4):
            for core in range(2):
                along_y = (core == 0) == first
                to_y = (y + shift) % 4 if along_y else y
                to_x = x if along_y else (x + shift) % 4
                pairs.append(((y * 4 + x) * 2 + core, (to_y * 4 + to_x) * 2 + core))
    return pairs


Z_PERMS = (
    [(z_index(z), z_index(z + 1)) for z in range(8)],
    [(z_index(z), z_index(z - 1)) for z in range(8)],
    [(z_index(z), z_index(z + 2 if z % 2 == 0 else z - 2)) for z in range(8)],
)


def send_three(block, axes, perms):
    return tuple(lax.ppermute(block, axes, perm) for perm in perms)


def attention_kernel(blocks_ref, counts_ref, qkv_ref, bias_ref, cos_ref, sin_ref, out_ref, q_scr, k_scr, v_scr):
    heads = q_scr.shape[0]
    cosine = cos_ref[...]
    sine = sin_ref[...]

    def rotated(column):
        value = qkv_ref[:, column : column + HEAD] + bias_ref[:, column : column + HEAD]
        return value * cosine + pltpu.roll(value, HEAD // 2, 1) * sine

    for head in range(heads):
        q_scr[head] = rotated(head * HEAD).astype(jnp.bfloat16)
    k_scr[...] = rotated(heads * HEAD).astype(jnp.bfloat16)
    start = (heads + 1) * HEAD
    v_scr[...] = (qkv_ref[:, start : start + HEAD] + bias_ref[:, start : start + HEAD]).astype(jnp.bfloat16)
    row = lax.broadcasted_iota(jnp.int32, (BLOCK, BLOCK), 0)
    column = lax.broadcasted_iota(jnp.int32, (BLOCK, BLOCK), 1)
    for head in range(heads):
        for block in range(4):
            query = q_scr[head, block * BLOCK : (block + 1) * BLOCK, :]
            count = counts_ref[head * 4 + block]
            total = jnp.zeros((BLOCK, 1), jnp.float32)
            mixed = jnp.zeros((BLOCK, HEAD), jnp.float32)
            for other in range(block + 1):
                keys = k_scr[other * BLOCK : (other + 1) * BLOCK, :]
                values = v_scr[other * BLOCK : (other + 1) * BLOCK, :]
                score = lax.dot_general(query, keys, (((1,), (1,)), ((), ())), preferred_element_type=jnp.float32)
                expo = jnp.exp(score * HEAD ** (-0.5))
                if other == block:
                    expo = jnp.where(column <= row, expo, 0.0)
                else:
                    seen = jnp.int32(0)
                    for slot in range(1, MAXB):
                        hit = (blocks_ref[(head * 4 + block) * MAXB + slot] == other) & (slot < count)
                        seen = seen | hit.astype(jnp.int32)
                    expo = jnp.where(seen > 0, expo, 0.0)
                total = total + jnp.sum(expo, axis=-1, keepdims=True)
                mixed = mixed + jnp.dot(expo.astype(jnp.bfloat16), values, preferred_element_type=jnp.float32)
            out_ref[block, :, head * HEAD : (head + 1) * HEAD] = (mixed / total).astype(jnp.bfloat16)


def attend(kv_blocks, block_counts, qkv, bias, cosine, sine):
    tokens = qkv.shape[0]
    heads = kv_blocks.shape[0]
    vmem = pl.BlockSpec(memory_space=pltpu.VMEM)
    smem = pl.BlockSpec(memory_space=pltpu.SMEM)
    return pl.pallas_call(
        attention_kernel,
        out_shape=jax.ShapeDtypeStruct((tokens // BLOCK, BLOCK, heads * HEAD), jnp.bfloat16),
        in_specs=[smem, smem, vmem, vmem, vmem, vmem],
        out_specs=vmem,
        scratch_shapes=[
            pltpu.VMEM((heads, tokens, HEAD), jnp.bfloat16),
            pltpu.VMEM((tokens, HEAD), jnp.bfloat16),
            pltpu.VMEM((tokens, HEAD), jnp.bfloat16),
        ],
        compiler_params=pltpu.CompilerParams(vmem_limit_bytes=32 * 1024 * 1024),
    )(kv_blocks.reshape(-1), block_counts.reshape(-1), qkv, bias, cosine, sine)


def rms_norm(tokens, norm_gain):
    floats = tokens.astype(jnp.float32)
    meansq = jnp.mean(floats * floats, axis=-1, keepdims=True)
    return (floats * lax.rsqrt(meansq + EPSILON) * norm_gain.astype(jnp.float32)).astype(jnp.bfloat16)


def rotary_tables(tokens):
    half = HEAD // 2
    exponent = jnp.arange(half, dtype=jnp.float32) * (2.0 / HEAD)
    inverse = jnp.power(jnp.float32(THETA), -exponent)
    angles = jnp.arange(tokens, dtype=jnp.float32)[:, None] * inverse[None, :]
    cosine = jnp.cos(angles)
    sine = jnp.sin(angles)
    return jnp.concatenate([cosine, cosine], axis=1), jnp.concatenate([-sine, sine], axis=1)


def body(hidden, norm_gain, w_query, w_key, w_value, bias_query, bias_key, bias_value, kv_blocks, block_counts):
    y, zl, x = (lax.axis_index(name) for name in DOC)
    zh, core = (lax.axis_index(name) for name in CTX)
    group = zh * 2 + core
    rows = w_query.shape[0]

    def own(weight, axis=1, group=group):
        width = weight.shape[axis] // 4
        return lax.dynamic_slice_in_dim(weight, group * width, width, axis)

    def columns_of(half):
        return jnp.concatenate([own(weight, 1, half * 2 + core) for weight in (w_query, w_key, w_value)], axis=1)

    bias = jnp.concatenate([own(bias_query, 0), own(bias_key, 0), own(bias_value, 0)])[None, :].astype(jnp.float32)

    z = zh * 4 + zl
    targets = (z + 1, z - 1, jnp.where(z % 2 == 0, z + 2, z - 2))
    shard = jnp.stack(
        [columns_of(zh)]
        + [
            lax.ppermute(columns_of((target % 8) // 4), ("zl", "zh"), perm)
            for target, perm in zip(targets, Z_PERMS, strict=True)
        ]
    )
    plane = ("y", "x", "core")
    first = [plane_perm(True, shift) for shift in (1, -1, 2)]
    second = [plane_perm(False, shift) for shift in (1, -1, 2)]
    shard = jnp.stack([shard, *send_three(shard, plane, first)])
    pieces = (shard, *send_three(shard, plane, second))

    normed = rms_norm(hidden[0], norm_gain)
    turned = normed.T.reshape(64, rows, BLOCK)
    offsets = jnp.array(OFFSETS, jnp.int32)
    ys, zs, xs = ((here + offsets) % 4 for here in (y, zl, x))
    index = (ys[:, None, None] * 4 + zs[None, None, :]) * 4 + xs[None, :, None]
    turned = turned[index.reshape(-1)].reshape(4, 4, 4 * rows, BLOCK)
    swap = lambda name, size: functools.partial(
        lax.ppermute, axis_name=name, perm=[(i, (i + 1) % size) for i in range(size)]
    )
    far = swap("zh", 2)(turned)
    near = swap("core", 2)(turned)
    far_near = swap("core", 2)(far)
    here_pair = jnp.stack([jnp.where(core == 0, turned, near), jnp.where(core == 0, near, turned)])
    far_pair = jnp.stack([jnp.where(core == 0, far, far_near), jnp.where(core == 0, far_near, far)])
    every = jnp.concatenate([jnp.where(zh == 0, here_pair, far_pair), jnp.where(zh == 0, far_pair, here_pair)])
    every = jnp.where(core == 0, every.transpose(0, 2, 1, 3, 4), every)
    summed = None
    for r, piece in enumerate(pieces):
        left = every[:, r].reshape(4, 4 * 4 * rows, BLOCK)
        part = lax.dot_general(
            left, piece.reshape(16 * rows, -1), (((1,), (0,)), ((), ())), preferred_element_type=jnp.float32
        )
        summed = part if summed is None else summed + part
    qkv = summed.reshape(4 * BLOCK, -1)
    cosine, sine = rotary_tables(4 * BLOCK)
    mixed = attend(kv_blocks, block_counts, qkv, bias, cosine, sine)
    back = lax.all_to_all(mixed, CTX, split_axis=0, concat_axis=0, tiled=True)
    return back.transpose(1, 0, 2).reshape(1, BLOCK, QHEADS * HEAD)


def solution(mesh):
    inner = Mesh(mesh.devices.reshape(4, 4, 4, 2, 2), AXES)
    rows = P(DOC, None)
    placed = (P(DOC, CTX, None), P(), rows, rows, rows, P(), P(), P(), P(CTX, None, None), P(CTX, None))
    return jax.shard_map(body, mesh=inner, in_specs=placed, out_specs=P(DOC, CTX, None), check_vma=False)
```
